32 devices in a mesh: section: 4 (over y, x), dp: 2 (over core), tensor: 4 (over z).
Axes of the slice: x: 2, y: 2, z: 4, core: 2. Of those that a mesh axis runs over, the one named last changes fastest.
Arguments:
- cotangent: bfloat16 [2, 256, 8192], P(None, 'dp', 'tensor'), may hold values from -6 to 6
- stash: bfloat16 [4, 2, 256, 8192], P('section', None, 'dp', 'tensor'), may hold values from -0.25 to 0.25
- factor_a: bfloat16 [4, 1024, 8192], P('section', 'dp', 'tensor'), may hold values from -0.0625 to 0.0625
- factor_b: bfloat16 [4, 8192, 1024], P('section', ('tensor', 'dp')), may hold values from -0.1875 to 0.1875
- block_vals: bfloat16 [4, 8, 128, 128], P('section', ('dp', 'tensor')), may hold values from -0.25 to 0.25
- block_rows: int32 [4, 8], P('section'), may hold values from 0 to 63, as said below
- block_cols: int32 [4, 8], P('section'), may hold values from 0 to 63, as said below
Outputs:
- grad_in: bfloat16 [4, 2, 256, 8192], P('section', None, 'dp', 'tensor')
- block_grad: float32 [4, 8, 128, 128], P('section', ('dp', 'tensor'))
The draws below stay inside these ranges and needn't reach their ends.
Inputs may be any that keep to these rules, and one draw needn't show every extreme that they name: The support lies inside the diagonal part of each tensor shard. Within a section all (block_rows, block_cols) pairs are distinct. For every dp index o < 2, tensor index t < 4 and slot k < 1, the block at position (o * 4 + t) + k has both its row and its column block index in [t * 8192 // (128 * 4), (t + 1) * 8192 // (128 * 4)). `block_cols`: drawn together with block_rows; the same promise holds.
All inputs are finite; a program needn't handle non-finite values.
Results may differ from the reference program's by a relative error of at most 0.024.
Values may be sent and summed in bfloat16 or wider, within the bound.
A program may use at most 128 MiB of HBM per device.

```python
import jax
import jax.numpy as jnp
from jax import lax

D = 8192
R = 1024
BS = 128
BLK = 1
M = 2
TOK_DEV = 128
TOKENS = 256
BLOCKS = 8
N_SECTION = 4
N_DP = 2
N_TENSOR = 4


def support_pairs(key):
    local_count = D // (BS * N_TENSOR)
    needed = N_DP * BLK
    base = jax.random.fold_in(key, 7)
    keys = jax.random.split(base, N_SECTION * N_TENSOR)
    picks = jax.vmap(lambda one_key: jax.random.permutation(one_key, local_count * local_count)[:needed])(keys)
    picks = picks.astype(jnp.int32).reshape(N_SECTION, N_TENSOR, N_DP, BLK).transpose(0, 2, 1, 3)
    offsets = jnp.arange(N_TENSOR, dtype=jnp.int32).reshape(1, 1, N_TENSOR, 1) * local_count
    row_ids = picks // local_count + offsets
    col_ids = picks % local_count + offsets
    return (row_ids.reshape(N_SECTION, -1).astype(jnp.int32), col_ids.reshape(N_SECTION, -1).astype(jnp.int32))


def draw_block_rows(key, part):
    return support_pairs(key)[0]


def draw_block_cols(key, part):
    return support_pairs(key)[1]


def level_of(stream_key, shape, cuts, low, top_value):
    def one(axis_at, shards_of):
        heights = jax.random.uniform(jax.random.fold_in(jax.random.fold_in(stream_key, 6), axis_at), (shards_of,), jnp.float32, low / len(cuts), top_value / len(cuts))
        return jnp.repeat(jnp.exp(heights), shape[axis_at] // shards_of).reshape((-1,) + (1,) * (len(shape) - axis_at - 1))

    factor_of = one(*cuts[0])
    for cut in cuts[1:]:
        factor_of = factor_of * one(*cut)
    return factor_of


def bell_draw(own_key, extent, width, bound, pieces=(), kind=jnp.bfloat16):
    factor_of = level_of(own_key, extent, pieces, -0.22, 0.18) if pieces else 1.0
    drawn = jax.random.normal(own_key, extent, jnp.float32) * width * factor_of
    return jnp.minimum(jnp.maximum(drawn, -bound), bound).astype(kind)


def setup_inputs(seed: int = 0) -> dict:
    key_of = jax.random.split(jax.random.key(seed), 8)
    return {
        "cotangent": bell_draw(key_of[0], (M, TOKENS, D), 1.0, 6.0, ((1, 2), (2, 4))),
        "stash": bell_draw(key_of[1], (N_SECTION, M, TOKENS, D), ((M * TOKENS) ** -0.5), 0.25, ((0, 4), (2, 2), (3, 4))),
        "factor_a": bell_draw(key_of[2], (N_SECTION, R, D), D ** -0.5, 0.0625, ((0, 4), (1, 2), (2, 4))),
        "factor_b": bell_draw(key_of[3], (N_SECTION, D, R), R ** -0.5, 0.1875, ((0, 4), (1, 8))),
        "block_vals": bell_draw(key_of[4], (N_SECTION, BLOCKS, BS, BS), (0.5 * BS ** -0.5), 0.25, ((0, 4), (1, 8))),
        "block_rows": draw_block_rows(jax.random.fold_in(key_of[7], 71), 0),
        "block_cols": draw_block_cols(jax.random.fold_in(key_of[7], 71), 0),
    }


def reference(cotangent, stash, factor_a, factor_b, block_vals, block_rows, block_cols):
    block_count = D // BS
    incoming = cotangent
    grads_in = [None] * N_SECTION
    grads_blocks = [None] * N_SECTION
    for section_idx in reversed(range(N_SECTION)):
        factor_left = factor_a[section_idx]
        factor_right = factor_b[section_idx]
        values = block_vals[section_idx].astype(jnp.float32)
        row_ids = block_rows[section_idx].astype(jnp.int32)
        col_ids = block_cols[section_idx].astype(jnp.int32)
        partial_grad = jnp.zeros((N_DP, BLOCKS, BS, BS), jnp.float32)
        outputs = []
        for batch_idx in range(M):
            cot_now = incoming[batch_idx]
            rank_act = jnp.dot(cot_now, factor_left.T, preferred_element_type=jnp.float32).astype(jnp.bfloat16)
            picked_cot = jnp.take(cot_now.reshape(TOKENS, block_count, BS), col_ids, axis=1).astype(jnp.float32)
            sparse_terms = jnp.einsum("tnc,nrc->tnr", picked_cot, values)
            sparse_grad = jnp.zeros((TOKENS, block_count, BS), jnp.float32).at[:, row_ids].add(sparse_terms)
            grad_out = jnp.dot(rank_act, factor_right.T, preferred_element_type=jnp.float32) + sparse_grad.reshape(TOKENS, D)
            outputs.append(grad_out.astype(jnp.bfloat16))
            picked_in = jnp.take(stash[section_idx, batch_idx].reshape(TOKENS, block_count, BS), row_ids, axis=1).astype(jnp.float32)
            partial_grad = partial_grad + jnp.einsum(
                "ptnr,ptnc->pnrc",
                picked_in.reshape(N_DP, TOK_DEV, BLOCKS, BS),
                picked_cot.reshape(N_DP, TOK_DEV, BLOCKS, BS),
            )
        rounded = lax.optimization_barrier(partial_grad.astype(jnp.bfloat16))
        grads_blocks[section_idx] = jnp.sum(rounded.astype(jnp.float32), axis=0)
        incoming = jnp.stack(outputs)
        grads_in[section_idx] = incoming
    return jnp.stack(grads_in), jnp.stack(grads_blocks)
```

```python
import functools

import jax
import jax.numpy as jnp
from jax import lax
from jax.experimental import pallas as pl
from jax.experimental.pallas import tpu as pltpu
from jax.sharding import PartitionSpec as P

PARTS = 2
WIDE = 512
MESH = pl.DeviceIdType.MESH
NT = (((1,), (1,)), ((), ()))
TN = (((0,), (0,)), ((), ()))


def dot(lhs, rhs, dims):
    return lax.dot_general(lhs, rhs, dims, preferred_element_type=jnp.float32)


def kernel(
    dims,
    cot, stash, fa, fb, bv, rows, cols,
    out, bg,
    u, a, b, v, st, acc, psend, rsb, rk, gs, sp, gacc, gsend, grecv,
    a_sem, b_sem, v_sem, st_sem, u_sem, us_sem, rs_sem, rr_sem, as_sem, ar_sem, o_sem, g_sem,
):
    sections, dp, tensor, paired = dims
    sec = lax.axis_index("section")
    dpi = lax.axis_index("dp")
    me = lax.axis_index("tensor")
    chunks, pieces, chunk, wide = u.shape
    bs = v.shape[-1]
    per = wide // bs
    local_blocks = pieces * per
    nblocks = v.shape[0]
    blk = nblocks // dp
    last = sections - 1

    barrier = pltpu.get_barrier_semaphore()

    def greet(axis, index):
        pl.semaphore_signal(barrier, inc=1, device_id={axis: index}, device_id_type=MESH)

    greet("section", lax.rem(sec + 1, sections))
    greet("section", lax.rem(sec + sections - 1, sections))
    for off in range(1, tensor):
        greet("tensor", lax.rem(me + off, tensor))
    if paired:
        greet("dp", 1 - dpi)

    def cot_copy(c, j):
        return pltpu.make_async_copy(
            cot.at[c, :, pl.ds(j * wide, wide)], u.at[c, j], u_sem.at[c, j]
        )

    @pl.when(sec == last)
    def _():
        def go(c, _):
            for j in range(pieces):
                cot_copy(c, j).start()
            return 0

        lax.fori_loop(0, chunks, go, 0)

    def share(src, dst, sem):
        if not paired:
            return [pltpu.make_async_copy(src, dst, sem.at[0])], None, None
        size = src.shape[0]
        mine = dst.at[pl.ds(dpi * size, size)]
        other = dst.at[pl.ds((1 - dpi) * size, size)]
        local = pltpu.make_async_copy(src, mine, sem.at[0])
        push = pltpu.make_async_remote_copy(
            src, mine, sem.at[1], sem.at[2], device_id={"dp": 1 - dpi}, device_id_type=MESH
        )
        pull = pltpu.make_async_remote_copy(
            src, other, sem.at[1], sem.at[2], device_id={"dp": 1 - dpi}, device_id_type=MESH
        )
        return [local], push, pull

    a_copy, b_copy, v_copy = share(fa, a, a_sem), share(fb, b, b_sem), share(bv, v, v_sem)
    st_copy = pltpu.make_async_copy(stash, st, st_sem)
    a_copy[0][0].start()
    pl.semaphore_wait(barrier, 2 + (tensor - 1) + (1 if paired else 0))
    if paired:
        a_copy[1].start()
    for one in (v_copy, b_copy):
        one[0][0].start()
        if paired:
            one[1].start()
    st_copy.start()
    gacc[...] = jnp.zeros_like(gacc)

    def arrive(one):
        one[0][0].wait()
        if paired:
            one[2].wait_recv()

    def rs_copy(c, src, k):
        return pltpu.make_async_remote_copy(
            psend.at[c, k], rsb.at[c, src], rs_sem.at[c, k], rr_sem.at[c, src],
            device_id={"tensor": k}, device_id_type=MESH,
        )

    def ag_copy(c, src, k):
        return pltpu.make_async_remote_copy(
            rk.at[c, src], rk.at[c, src], as_sem.at[c, k], ar_sem.at[c, src],
            device_id={"tensor": k}, device_id_type=MESH,
        )

    def hop_copy(c, j):
        return pltpu.make_async_remote_copy(
            gs.at[c, j], u.at[c, j], us_sem.at[c, j], u_sem.at[c, j],
            device_id={"section": lax.rem(sec + sections - 1, sections)}, device_id_type=MESH,
        )

    def out_copy(c, j):
        return pltpu.make_async_copy(
            gs.at[c, j], out.at[c, :, pl.ds(j * wide, wide)], o_sem.at[c, j]
        )

    def place(n):
        return (n // blk * tensor + me) * blk + n % blk

    def project(c):
        for j in range(pieces):

            @pl.when(sec == last)
            def _():
                cot_copy(c, j).wait()

            @pl.when(sec != last)
            def _():
                hop_copy(c, j).wait_recv()

            piece = u[c, j]
            span = acc.shape[-1]
            for k in range(tensor):
                term = dot(piece, a[k * span : (k + 1) * span, j * wide : (j + 1) * wide], NT)
                if j > 0:
                    term = acc[k] + term
                acc[k] = term
                if j == pieces - 1:
                    psend[c, k] = term.astype(jnp.bfloat16)

                    @pl.when(me != k)
                    def _():
                        rs_copy(c, me, k).start()

    def sparse(c):
        def one(n, _):
            row = rows[0, place(n)] - me * local_blocks
            col = cols[0, place(n)] - me * local_blocks
            rows_at = jnp.full((chunk, bs), row, jnp.int32)
            cols_at = jnp.full((chunk, bs), col, jnp.int32)
            picked = jnp.zeros((chunk, bs), jnp.float32)
            inner = jnp.zeros((chunk, bs), jnp.float32)
            for at in range(local_blocks):
                here = at % per * bs
                seen = u[c, at // per, :, here : here + bs].astype(jnp.float32)
                picked = jnp.where(cols_at == at, seen, picked)
                held = st[c, :, at * bs : (at + 1) * bs].astype(jnp.float32)
                inner = jnp.where(rows_at == at, held, inner)
            picked = picked.astype(jnp.bfloat16)
            sp[c, n] = dot(picked, v[n], NT)
            gacc[n] += dot(inner.astype(jnp.bfloat16), picked, TN)
            return 0

        lax.fori_loop(0, nblocks, one, 0, unroll=nblocks <= 4)

    def reduce(c):
        total = acc[me]
        for off in range(1, tensor):
            src = lax.rem(me + off, tensor)
            rs_copy(c, src, src).wait_recv()
            total = total + rsb[c, src].astype(jnp.float32)
        rk[c, me] = total.astype(jnp.bfloat16)
        for off in range(1, tensor):
            ag_copy(c, me, lax.rem(me + off, tensor)).start()

    def expand(c):
        for off in range(1, tensor):
            src = lax.rem(me + off, tensor)
            ag_copy(c, src, src).wait_recv()
        rank = jnp.concatenate([rk[c, k] for k in range(tensor)], axis=1)
        lane = lax.broadcasted_iota(jnp.int32, (chunk, wide), 1) // bs
        for j in range(pieces):
            dense = dot(rank, b[j * wide : (j + 1) * wide, :], NT)

            def one(n, total):
                row = rows[0, place(n)] - me * local_blocks - j * per
                tiled = jnp.concatenate([sp[c, n]] * per, axis=1)
                return total + jnp.where(lane == row, tiled, 0.0)

            total = lax.fori_loop(0, nblocks, one, jnp.zeros_like(dense), unroll=nblocks <= 4)
            gs[c, j] = (dense + total).astype(jnp.bfloat16)

            @pl.when(sec > 0)
            def _():
                hop_copy(c, j).start()

            out_copy(c, j).start()

    arrive(a_copy)

    def step(i, _):
        @pl.when(i < chunks)
        def _():
            project(i)

            @pl.when(i == 0)
            def _():
                arrive(v_copy)
                st_copy.wait()

            sparse(i)

        @pl.when(i == 1)
        def _():
            arrive(b_copy)

        @pl.when(i > 0)
        def _():
            expand(i - 1)

        @pl.when(i < chunks)
        def _():
            reduce(i)

        return 0

    lax.fori_loop(0, chunks + 1, step, 0)

    if paired:
        gsend[...] = gacc[pl.ds((1 - dpi) * blk, blk)].astype(jnp.bfloat16)
        swap = pltpu.make_async_remote_copy(
            gsend, grecv, g_sem.at[0], g_sem.at[1], device_id={"dp": 1 - dpi}, device_id_type=MESH
        )
        swap.start()
    else:
        bg[...] = gacc[...].astype(bg.dtype)

    def drain(c, _):
        for off in range(1, tensor):
            dst = lax.rem(me + off, tensor)
            rs_copy(c, me, dst).wait_send()
            ag_copy(c, me, dst).wait_send()
        for j in range(pieces):

            @pl.when(sec > 0)
            def _():
                hop_copy(c, j).wait_send()

            out_copy(c, j).wait()
        return 0

    lax.fori_loop(0, chunks, drain, 0)
    if paired:
        for one in (a_copy, v_copy, b_copy):
            one[1].wait_send()
        swap.wait()
        kept = gacc[pl.ds(dpi * blk, blk)].astype(jnp.bfloat16).astype(jnp.float32)
        bg[...] = kept + grecv[...].astype(jnp.float32)


def on_device(cotangent, stash, factor_a, factor_b, block_vals, block_rows, block_cols):
    sections = lax.axis_size("section")
    dp = lax.axis_size("dp")
    tensor = lax.axis_size("tensor")
    paired = dp == 2
    _, batches, tokens, width = stash.shape
    rank = factor_b.shape[-1]
    blk, bs = block_vals.shape[1:3]
    parts = [factor_a[0], factor_b[0], block_vals[0]]
    if not paired:
        parts = [lax.all_gather(part, "dp", axis=0, tiled=True) for part in parts]
    nblocks = dp * blk
    chunks, chunk = batches * PARTS, tokens // PARTS
    wide = min(WIDE, width)
    pieces = width // wide
    span = rank // tensor
    bf, f32 = jnp.bfloat16, jnp.float32
    vmem, dma = pltpu.VMEM, pltpu.SemaphoreType.DMA
    hbm = pl.BlockSpec(memory_space=pl.ANY)
    smem = pl.BlockSpec(memory_space=pltpu.SMEM)
    grads, blocks = pl.pallas_call(
        functools.partial(kernel, (sections, dp, tensor, paired)),
        out_shape=(
            jax.ShapeDtypeStruct((chunks, chunk, width), bf),
            jax.ShapeDtypeStruct((blk if paired else nblocks, bs, bs), f32 if paired else bf),
        ),
        in_specs=[hbm] * 5 + [smem] * 2,
        out_specs=(hbm, pl.BlockSpec(memory_space=vmem)),
        scratch_shapes=[
            vmem((chunks, pieces, chunk, wide), bf),
            vmem((rank, width), bf),
            vmem((width, rank), bf),
            vmem((nblocks, bs, bs), bf),
            vmem((chunks, chunk, width), bf),
            vmem((tensor, chunk, span), f32),
            vmem((chunks, tensor, chunk, span), bf),
            vmem((chunks, tensor, chunk, span), bf),
            vmem((chunks, tensor, chunk, span), bf),
            vmem((chunks, pieces, chunk, wide), bf),
            vmem((chunks, nblocks, chunk, bs), f32),
            vmem((nblocks, bs, bs), f32),
            vmem((blk, bs, bs), bf),
            vmem((blk, bs, bs), bf),
            dma((3,)),
            dma((3,)),
            dma((3,)),
            dma,
            dma((chunks, pieces)),
            dma((chunks, pieces)),
            dma((chunks, tensor)),
            dma((chunks, tensor)),
            dma((chunks, tensor)),
            dma((chunks, tensor)),
            dma((chunks, pieces)),
            dma((2,)),
        ],
        compiler_params=pltpu.CompilerParams(
            collective_id=0, has_side_effects=True, vmem_limit_bytes=48 << 20
        ),
    )(
        cotangent.reshape(chunks, chunk, width),
        stash.reshape(chunks, chunk, width),
        *parts,
        block_rows,
        block_cols,
    )
    if not paired:
        blocks = lax.psum_scatter(blocks, "dp", scatter_dimension=0, tiled=True).astype(f32)
    return grads.reshape(stash.shape), blocks[None]


def solution(mesh):
    in_specs = (
        P(None, "dp", "tensor"),
        P("section", None, "dp", "tensor"),
        P("section", "dp", "tensor"),
        P("section", ("tensor", "dp"), None),
        P("section", ("dp", "tensor"), None, None),
        P("section", None),
        P("section", None),
    )
    out_specs = (P("section", None, "dp", "tensor"), P("section", ("dp", "tensor"), None, None))
    return jax.shard_map(
        on_device, mesh=mesh, in_specs=in_specs, out_specs=out_specs, check_vma=False
    )
```

```python
import functools

import jax
import jax.numpy as jnp
from jax import lax
from jax.experimental import pallas as pl
from jax.experimental.pallas import tpu as pltpu
from jax.sharding import PartitionSpec as P

PARTS = 4
SUM_LAG = 1
OUT_LAG = 2
WIDE = 512
MESH = pl.DeviceIdType.MESH
NT = (((1,), (1,)), ((), ()))
NN = (((1,), (0,)), ((), ()))
TN = (((0,), (0,)), ((), ()))


def dot(lhs, rhs, dims):
    return lax.dot_general(lhs, rhs, dims, preferred_element_type=jnp.float32)


def kernel(
    dims,
    cot, stash, fa, fb, bv, rows, cols,
    out, bg,
    u, a, b, at, bt, v, st, acc, psend, rsb, rk, gs, sp, gacc, gsend, grecv,
    a_sem, b_sem, v_sem, st_sem, u_sem, us_sem, rs_sem, rr_sem, as_sem, ar_sem, o_sem, g_sem,
):
    sections, dp, tensor, paired = dims
    sec = lax.axis_index("section")
    dpi = lax.axis_index("dp")
    me = lax.axis_index("tensor")
    chunks, pieces, chunk, wide = u.shape
    bs = v.shape[-1]
    per = wide // bs
    local_blocks = pieces * per
    nblocks = v.shape[0]
    blk = nblocks // dp
    last = sections - 1

    barrier = pltpu.get_barrier_semaphore()

    def greet(axis, index):
        pl.semaphore_signal(barrier, inc=1, device_id={axis: index}, device_id_type=MESH)

    greet("section", lax.rem(sec + 1, sections))
    greet("section", lax.rem(sec + sections - 1, sections))
    for off in range(1, tensor):
        greet("tensor", lax.rem(me + off, tensor))
    if paired:
        greet("dp", 1 - dpi)

    def cot_copy(c, j):
        return pltpu.make_async_copy(
            cot.at[c, :, pl.ds(j * wide, wide)], u.at[c, j], u_sem.at[c, j]
        )

    @pl.when(sec == last)
    def _():
        def go(c, _):
            for j in range(pieces):
                cot_copy(c, j).start()
            return 0

        lax.fori_loop(0, chunks, go, 0)

    def share(src, dst, sem):
        if not paired:
            return [pltpu.make_async_copy(src, dst, sem.at[0])], None, None
        size = src.shape[0]
        mine = dst.at[pl.ds(dpi * size, size)]
        other = dst.at[pl.ds((1 - dpi) * size, size)]
        local = pltpu.make_async_copy(src, mine, sem.at[0])
        push = pltpu.make_async_remote_copy(
            src, mine, sem.at[1], sem.at[2], device_id={"dp": 1 - dpi}, device_id_type=MESH
        )
        pull = pltpu.make_async_remote_copy(
            src, other, sem.at[1], sem.at[2], device_id={"dp": 1 - dpi}, device_id_type=MESH
        )
        return [local], push, pull

    a_copy, b_copy, v_copy = share(fa, a, a_sem), share(fb, b, b_sem), share(bv, v, v_sem)
    st_copy = pltpu.make_async_copy(stash, st, st_sem)
    a_copy[0][0].start()
    pl.semaphore_wait(barrier, 2 + (tensor - 1) + (1 if paired else 0))
    if paired:
        a_copy[1].start()
    v_copy[0][0].start()
    if paired:
        v_copy[1].start()
    st_copy.start()
    gacc[...] = jnp.zeros_like(gacc)

    def arrive(one):
        one[0][0].wait()
        if paired:
            one[2].wait_recv()

    def rs_copy(c, src, k):
        return pltpu.make_async_remote_copy(
            psend.at[c, k], rsb.at[c, src], rs_sem.at[c, k], rr_sem.at[c, src],
            device_id={"tensor": k}, device_id_type=MESH,
        )

    def ag_copy(c, src, k):
        return pltpu.make_async_remote_copy(
            rk.at[c, src], rk.at[c, src], as_sem.at[c, k], ar_sem.at[c, src],
            device_id={"tensor": k}, device_id_type=MESH,
        )

    def hop_copy(c, j):
        return pltpu.make_async_remote_copy(
            gs.at[c, j], u.at[c, j], us_sem.at[c, j], u_sem.at[c, j],
            device_id={"section": lax.rem(sec + sections - 1, sections)}, device_id_type=MESH,
        )

    def out_copy(c, j):
        return pltpu.make_async_copy(
            gs.at[c, j], out.at[c, :, pl.ds(j * wide, wide)], o_sem.at[c, j]
        )

    def place(n):
        return (n // blk * tensor + me) * blk + n % blk

    def project(c, turned):
        for j in range(pieces):
            if turned:
                hop_copy(c, j).wait_recv()
            else:
                cot_copy(c, j).wait()
            piece = u[c, j]
            span = acc.shape[-1]
            for k in range(tensor):
                ranks, columns = pl.ds(k * span, span), pl.ds(j * wide, wide)
                if turned:
                    term = dot(piece, at[columns, ranks], NN)
                else:
                    term = dot(piece, a[ranks, columns], NT)
                if j > 0:
                    term = acc[c % acc.shape[0], k] + term
                acc[c % acc.shape[0], k] = term
                if j == pieces - 1:
                    psend[c, k] = term.astype(jnp.bfloat16)

                    @pl.when(me != k)
                    def _():
                        rs_copy(c, me, k).start()

    def sparse(c):
        def one(n, _):
            row = rows[0, place(n)] - me * local_blocks
            col = cols[0, place(n)] - me * local_blocks
            rows_at = jnp.full((chunk, bs), row, jnp.int32)
            cols_at = jnp.full((chunk, bs), col, jnp.int32)
            picked = jnp.zeros((chunk, bs), jnp.float32)
            inner = jnp.zeros((chunk, bs), jnp.float32)
            for at in range(local_blocks):
                here = at % per * bs
                seen = u[c, at // per, :, here : here + bs].astype(jnp.float32)
                picked = jnp.where(cols_at == at, seen, picked)
                held = st[c, :, at * bs : (at + 1) * bs].astype(jnp.float32)
                inner = jnp.where(rows_at == at, held, inner)
            picked = picked.astype(jnp.bfloat16)
            sp[c, n] = dot(picked, v[n], NT)
            gacc[n] += dot(inner.astype(jnp.bfloat16), picked, TN)
            return 0

        lax.fori_loop(0, nblocks, one, 0, unroll=nblocks <= 4)

    def reduce(c):
        total = acc[c % acc.shape[0], me]
        for off in range(1, tensor):
            src = lax.rem(me + off, tensor)
            rs_copy(c, src, src).wait_recv()
            total = total + rsb[c, src].astype(jnp.float32)
        rk[c, me] = total.astype(jnp.bfloat16)
        for off in range(1, tensor):
            ag_copy(c, me, lax.rem(me + off, tensor)).start()

    def expand(c, turned):
        for off in range(1, tensor):
            src = lax.rem(me + off, tensor)
            ag_copy(c, src, src).wait_recv()
        rank = jnp.concatenate([rk[c, k] for k in range(tensor)], axis=1)
        lane = lax.broadcasted_iota(jnp.int32, (chunk, wide), 1) // bs
        for j in range(pieces):
            if turned:
                dense = dot(rank, bt[:, j * wide : (j + 1) * wide], NN)
            else:
                dense = dot(rank, b[j * wide : (j + 1) * wide, :], NT)

            def one(n, total):
                row = rows[0, place(n)] - me * local_blocks - j * per
                tiled = jnp.concatenate([sp[c, n]] * per, axis=1)
                return total + jnp.where(lane == row, tiled, 0.0)

            total = lax.fori_loop(0, nblocks, one, jnp.zeros_like(dense), unroll=nblocks <= 4)
            gs[c, j] = (dense + total).astype(jnp.bfloat16)

            if turned:

                @pl.when(sec > 0)
                def _():
                    hop_copy(c, j).start()

            else:
                hop_copy(c, j).start()

            out_copy(c, j).start()

    arrive(a_copy)
    b_copy[0][0].start()
    if paired:
        b_copy[1].start()

    @pl.when(sec != last)
    def _():
        def turn(src, dst):
            height, length = src.shape
            tile = min(height, length, 256)

            def go(n, _):
                top = pl.multiple_of(n * tile, tile)
                for x in range(0, length, tile):
                    dst[x : x + tile, pl.ds(top, tile)] = src[pl.ds(top, tile), x : x + tile].T
                return 0

            lax.fori_loop(0, height // tile, go, 0)

        turn(a, at)
        arrive(b_copy)
        turn(b, bt)

    def step(i, _):
        @pl.when(i < chunks)
        def _():
            @pl.when(sec == last)
            def _():
                project(i, False)

            @pl.when(sec != last)
            def _():
                project(i, True)


        @pl.when((i >= SUM_LAG) & (i < chunks + SUM_LAG))
        def _():
            reduce(i - SUM_LAG)

        @pl.when(i < chunks)
        def _():
            @pl.when(i == 0)
            def _():
                arrive(v_copy)
                st_copy.wait()

            sparse(i)

        @pl.when((i >= OUT_LAG) & (sec == last))
        def _():
            @pl.when(i == OUT_LAG)
            def _():
                arrive(b_copy)

            expand(i - OUT_LAG, False)

        @pl.when((i >= OUT_LAG) & (sec != last))
        def _():
            expand(i - OUT_LAG, True)

        return 0

    lax.fori_loop(0, chunks + OUT_LAG, step, 0)

    if paired:
        gsend[...] = gacc[pl.ds((1 - dpi) * blk, blk)].astype(jnp.bfloat16)
        swap = pltpu.make_async_remote_copy(
            gsend, grecv, g_sem.at[0], g_sem.at[1], device_id={"dp": 1 - dpi}, device_id_type=MESH
        )
        swap.start()
    else:
        bg[...] = gacc[...].astype(bg.dtype)

    def drain(c, _):
        for off in range(1, tensor):
            dst = lax.rem(me + off, tensor)
            rs_copy(c, me, dst).wait_send()
            ag_copy(c, me, dst).wait_send()
        for j in range(pieces):

            @pl.when(sec > 0)
            def _():
                hop_copy(c, j).wait_send()

            out_copy(c, j).wait()
        return 0

    lax.fori_loop(0, chunks, drain, 0)
    if paired:
        for one in (a_copy, v_copy, b_copy):
            one[1].wait_send()
        swap.wait()
        kept = gacc[pl.ds(dpi * blk, blk)].astype(jnp.bfloat16).astype(jnp.float32)
        bg[...] = kept + grecv[...].astype(jnp.float32)


def on_device(cotangent, stash, factor_a, factor_b, block_vals, block_rows, block_cols):
    sections = lax.axis_size("section")
    dp = lax.axis_size("dp")
    tensor = lax.axis_size("tensor")
    paired = dp == 2
    _, batches, tokens, width = stash.shape
    rank = factor_b.shape[-1]
    blk, bs = block_vals.shape[1:3]
    parts = [factor_a[0], factor_b[0], block_vals[0]]
    if not paired:
        parts = [lax.all_gather(part, "dp", axis=0, tiled=True) for part in parts]
    nblocks = dp * blk
    chunks, chunk = batches * PARTS, tokens // PARTS
    wide = min(WIDE, width)
    pieces = width // wide
    span = rank // tensor
    bf, f32 = jnp.bfloat16, jnp.float32
    vmem, dma = pltpu.VMEM, pltpu.SemaphoreType.DMA
    hbm = pl.BlockSpec(memory_space=pltpu.HBM)
    smem = pl.BlockSpec(memory_space=pltpu.SMEM)
    grads, blocks = pl.pallas_call(
        functools.partial(kernel, (sections, dp, tensor, paired)),
        out_shape=(
            jax.ShapeDtypeStruct((chunks, chunk, width), bf),
            jax.ShapeDtypeStruct((blk if paired else nblocks, bs, bs), f32 if paired else bf),
        ),
        in_specs=[hbm] * 5 + [smem] * 2,
        out_specs=(hbm, pl.BlockSpec(memory_space=vmem)),
        scratch_shapes=[
            vmem((chunks, pieces, chunk, wide), bf),
            vmem((rank, width), bf),
            vmem((width, rank), bf),
            vmem((width, rank), bf),
            vmem((rank, width), bf),
            vmem((nblocks, bs, bs), bf),
            vmem((chunks, chunk, width), bf),
            vmem((SUM_LAG + 1, tensor, chunk, span), f32),
            vmem((chunks, tensor, chunk, span), bf),
            vmem((chunks, tensor, chunk, span), bf),
            vmem((chunks, tensor, chunk, span), bf),
            vmem((chunks, pieces, chunk, wide), bf),
            vmem((chunks, nblocks, chunk, bs), f32),
            vmem((nblocks, bs, bs), f32),
            vmem((blk, bs, bs), bf),
            vmem((blk, bs, bs), bf),
            dma((3,)),
            dma((3,)),
            dma((3,)),
            dma,
            dma((chunks, pieces)),
            dma((chunks, pieces)),
            dma((chunks, tensor)),
            dma((chunks, tensor)),
            dma((chunks, tensor)),
            dma((chunks, tensor)),
            dma((chunks, pieces)),
            dma((2,)),
        ],
        compiler_params=pltpu.CompilerParams(
            collective_id=0, has_side_effects=True, vmem_limit_bytes=60 << 20
        ),
    )(
        cotangent.reshape(chunks, chunk, width),
        stash.reshape(chunks, chunk, width),
        *parts,
        block_rows,
        block_cols,
    )
    if not paired:
        blocks = lax.psum_scatter(blocks, "dp", scatter_dimension=0, tiled=True).astype(f32)
    return grads.reshape(stash.shape), blocks[None]


def solution(mesh):
    in_specs = (
        P(None, "dp", "tensor"),
        P("section", None, "dp", "tensor"),
        P("section", "dp", "tensor"),
        P("section", ("tensor", "dp"), None),
        P("section", ("dp", "tensor"), None, None),
        P("section", None),
        P("section", None),
    )
    out_specs = (P("section", None, "dp", "tensor"), P("section", ("dp", "tensor"), None, None))
    return jax.shard_map(
        on_device, mesh=mesh, in_specs=in_specs, out_specs=out_specs, check_vma=False
    )
```
